32 devices in a mesh: dp: 2 (over y), fsdp: 16 (over z, x, core).
Axes of the slice: x: 2, y: 2, z: 4, core: 2. Of those that a mesh axis runs over, the one named last changes fastest.
Arguments:
- tokens: bfloat16 [32768, 768], P(('dp', 'fsdp')), may hold values from -6 to 6
- lengths: int32 [32], P(('dp', 'fsdp')), may hold values from 512 to 1024, as said below
- rand_blocks: int32 [32, 14, 12, 3], P(('dp', 'fsdp')), may hold values from 0 to 15
- cotangent: bfloat16 [32768, 768], P(('dp', 'fsdp')), may hold values from -6 to 6
- first_gain: bfloat16 [768], P(('dp', 'fsdp')), may hold values from 0.25 to 1.75
- first_shift: bfloat16 [768], P(('dp', 'fsdp')), may hold values from -1 to 1
- query_weight: bfloat16 [768, 768], P(('dp', 'fsdp')), may hold values from -0.4375 to 0.4375
- query_bias: bfloat16 [768], P(('dp', 'fsdp')), may hold values from -1 to 1
- key_weight: bfloat16 [768, 768], P(('dp', 'fsdp')), may hold values from -0.21875 to 0.21875
- value_weight: bfloat16 [768, 768], P(('dp', 'fsdp')), may hold values from -0.21875 to 0.21875
- value_bias: bfloat16 [768], P(('dp', 'fsdp')), may hold values from -1 to 1
- out_weight: bfloat16 [768, 768], P(('dp', 'fsdp')), may hold values from -0.875 to 0.875
- out_bias: bfloat16 [768], P(('dp', 'fsdp')), may hold values from -1 to 1
- second_gain: bfloat16 [768], P(('dp', 'fsdp')), may hold values from 0.25 to 1.75
- second_shift: bfloat16 [768], P(('dp', 'fsdp')), may hold values from -1 to 1
- up_weight: bfloat16 [768, 3072], P(('dp', 'fsdp')), may hold values from -0.21875 to 0.21875
- up_bias: bfloat16 [3072], P(('dp', 'fsdp')), may hold values from -1 to 1
- down_weight: bfloat16 [3072, 768], P(('dp', 'fsdp')), may hold values from -0.109375 to 0.109375
- down_bias: bfloat16 [768], P(('dp', 'fsdp')), may hold values from -1 to 1
Outputs:
- layer_out: bfloat16 [32768, 768], P(('dp', 'fsdp'))
- input_grad: float32 [32768, 768], P(('dp', 'fsdp'))
- first_gain_grad: float32 [768], P(('dp', 'fsdp'))
- first_shift_grad: float32 [768], P(('dp', 'fsdp'))
- query_weight_grad: float32 [768, 768], P(('dp', 'fsdp'))
- query_bias_grad: float32 [768], P(('dp', 'fsdp'))
- key_weight_grad: float32 [768, 768], P(('dp', 'fsdp'))
- value_weight_grad: float32 [768, 768], P(('dp', 'fsdp'))
- value_bias_grad: float32 [768], P(('dp', 'fsdp'))
- out_weight_grad: float32 [768, 768], P(('dp', 'fsdp'))
- out_bias_grad: float32 [768], P(('dp', 'fsdp'))
- second_gain_grad: float32 [768], P(('dp', 'fsdp'))
- second_shift_grad: float32 [768], P(('dp', 'fsdp'))
- up_weight_grad: float32 [768, 3072], P(('dp', 'fsdp'))
- up_bias_grad: float32 [3072], P(('dp', 'fsdp'))
- down_weight_grad: float32 [3072, 768], P(('dp', 'fsdp'))
- down_bias_grad: float32 [768], P(('dp', 'fsdp'))
The draws below stay inside these ranges and needn't reach their ends.
Inputs may be any that keep to these rules, and one draw needn't show every extreme that they name: `lengths`: the live tokens of each window come first; the other slots of its 1024 are padding; some window has all 1024 live. `rand_blocks`: block numbers within the window.
All inputs are finite; a program needn't handle non-finite values.
Results may differ from the reference program's by a relative error of at most 0.02.
Values may be sent and summed in bfloat16 or wider, within the bound.
A program may use at most 256 MiB of HBM per device.

```python
import jax
import jax.numpy as jnp
from jax import lax

D = 768
H = 12
HD = 64
FF = 3072
BLK = 64
NBLK = 16
LMAX = 1024
SEQS = 32
TOKENS = 32768


def draw_lengths(key, part):
    drawn = jax.random.randint(key, (SEQS,), LMAX // 2, LMAX + 1)
    return drawn.at[0].set(LMAX).astype(jnp.int32)


def set_ends(values, key, least, largest):
    spot = [jax.random.randint(jax.random.fold_in(key, axis), (), 0, length) for axis, length in enumerate(values.shape)]
    longest = values.shape.index(max(values.shape))
    next_to = spot[:longest] + [(spot[longest] + 1) % values.shape[longest]] + spot[longest + 1:]
    return values.at[tuple(spot)].set(least).at[tuple(next_to)].set(largest)


def raised(values, rng, source, target, parts, factor):
    owner, partner = [(jnp.arange(values.shape[dim]) // (values.shape[dim] // parts)).reshape([-1 if axis == dim else 1 for axis in range(values.ndim)]) for dim in (source, target)]
    chosen = jax.random.permutation(rng, parts)[partner]
    strong = (owner == chosen) | (owner == (partner + parts // 2) % parts)
    return jnp.where(strong, factor * values, values)


def level_of(rng, dims, cuts, smallest, high):
    level, own = 1.0, jax.random.fold_in(rng, 6)
    for axis_at, blocks in cuts:
        draws = jnp.exp(jax.random.uniform(jax.random.fold_in(own, axis_at), (blocks,), jnp.float32, smallest / len(cuts), high / len(cuts)))
        level = level * jnp.repeat(draws, dims[axis_at] // blocks).reshape([-1 if axis == axis_at else 1 for axis in range(len(dims))])
    return level


def scatter_about(stream_key, shape, width, bound, shards=(), kind=jnp.bfloat16):
    values = width * jax.random.normal(stream_key, shape, jnp.float32)
    if shards:
        values = values * level_of(stream_key, shape, shards, -0.22, 0.18)
    return jnp.clip(values, -bound, bound).astype(kind)


def gaussian_with(own_key, shape, deviation, reach, split, heavy, kind=jnp.bfloat16):
    result = deviation * jax.random.normal(own_key, shape, jnp.float32)
    if split:
        result = result * level_of(own_key, shape, split, -0.22, 0.18)
    return jnp.clip(raised(result, jax.random.fold_in(own_key, 3), *heavy), -reach, reach).astype(kind)


def setup_inputs(seed: int = 0) -> dict:
    key_of = jax.random.split(jax.random.key(seed), 20)
    return {
        "tokens": gaussian_with(key_of[0], (TOKENS, D), 1.0, 6.0, ((0, 32),), (0, 1, 32, 2.75)),
        "lengths": draw_lengths(jax.random.fold_in(key_of[19], 71), 0),
        "rand_blocks": set_ends(jax.random.randint(key_of[2], (SEQS, NBLK - 2, H, 3), 0, NBLK), jax.random.fold_in(key_of[2], 1), 0, NBLK - 1).astype(jnp.int32),
        "cotangent": gaussian_with(key_of[3], (TOKENS, D), 1.0, 6.0, ((0, 32),), (0, 1, 32, 2.75)),
        "first_gain": jnp.clip(1.0 + 0.15 * jax.random.normal(key_of[4], (D,), jnp.float32), 0.25, 1.75).astype(jnp.bfloat16),
        "first_shift": scatter_about(key_of[5], (D,), 0.2, 1.0, ((0, 32),)),
        "query_weight": scatter_about(key_of[6], (D, D), (D // 4) ** -0.5, 0.4375, ((0, 32),)),
        "query_bias": scatter_about(key_of[7], (D,), 0.2, 1.0, ((0, 32),)),
        "key_weight": scatter_about(key_of[8], (D, D), D ** -0.5, 0.21875, ((0, 32),)),
        "value_weight": scatter_about(key_of[9], (D, D), D ** -0.5, 0.21875, ((0, 32),)),
        "value_bias": scatter_about(key_of[10], (D,), 0.2, 1.0, ((0, 32),)),
        "out_weight": scatter_about(key_of[11], (D, D), (D // 16) ** -0.5, 0.875, ((0, 32),)),
        "out_bias": scatter_about(key_of[12], (D,), 0.2, 1.0, ((0, 32),)),
        "second_gain": jnp.clip(1.0 + 0.15 * jax.random.normal(key_of[13], (D,), jnp.float32), 0.25, 1.75).astype(jnp.bfloat16),
        "second_shift": scatter_about(key_of[14], (D,), 0.2, 1.0, ((0, 32),)),
        "up_weight": scatter_about(key_of[15], (D, FF), D ** -0.5, 0.21875, ((0, 32),)),
        "up_bias": scatter_about(key_of[16], (FF,), 0.2, 1.0, ((0, 32),)),
        "down_weight": scatter_about(key_of[17], (FF, D), FF ** -0.5, 0.109375, ((0, 32),)),
        "down_bias": scatter_about(key_of[18], (D,), 0.2, 1.0, ((0, 32),)),
    }


@jax.custom_vjp
def low(v):
    return lax.optimization_barrier(v.astype(jnp.bfloat16)).astype(jnp.float32)

@jax.custom_vjp
def low_back(v):
    return v

def low_keep(v):
    return (low(v), None)

def low_pass(kept, grad):
    return (grad,)

def back_keep(v):
    return (v, None)

def back_low(kept, grad):
    return (low(grad),)
low.defvjp(low_keep, low_pass)
low_back.defvjp(back_keep, back_low)
masked_fill = -1e+30
highest = lax.Precision.HIGHEST

def layer_norm(values, gain, shift):
    centre = lax.optimization_barrier(jnp.mean(values, axis=-1, keepdims=True))
    centred = values - centre
    inverse = lax.rsqrt(lax.optimization_barrier(jnp.mean(centred * centred, axis=-1, keepdims=True)) + 1e-05)
    return centred * inverse * gain + shift

def product(left, right):
    return jnp.dot(left, right, precision=highest)

def block_lists(rand_rows, count):
    later = jnp.arange(2, count, dtype=jnp.int32)
    fixed = jnp.stack([jnp.zeros_like(later), jnp.ones_like(later), later - 1, later, later + 1], axis=-1)
    fixed = jnp.broadcast_to(fixed[:, None, :], (count - 2, rand_rows.shape[1], 5))
    return jnp.concatenate([fixed, rand_rows.astype(jnp.int32)], axis=-1)

def window_layer(window, length, rand_rows, params):
    first_gain, first_shift, query_weight, query_bias, key_weight, value_weight, value_bias, out_weight, out_bias, second_gain, second_shift, up_weight, up_bias, down_weight, down_bias = params
    token_count = window.shape[0]
    front = 2 * BLK
    key_live = jnp.arange(token_count) < length
    normed = low(layer_norm(window, first_gain, first_shift))
    query_flat = low_back(low((product(normed, query_weight) + query_bias) * 0.125))
    key_flat = low_back(low(product(normed, key_weight)))
    value_flat = low_back(low(product(normed, value_weight) + value_bias))
    query_heads = query_flat.reshape(token_count, H, HD)
    key_heads = key_flat.reshape(token_count, H, HD)
    value_heads = value_flat.reshape(token_count, H, HD)
    global_scores = low_back(jnp.einsum('qhd,khd->hqk', query_heads[:front], key_heads, precision=highest))
    global_scores = jnp.where(key_live[None, None, :], global_scores, masked_fill)
    global_probs = low(jax.nn.softmax(global_scores, axis=-1))
    global_out = jnp.einsum('hqk,khd->qhd', global_probs, value_heads, precision=highest)
    chosen = block_lists(rand_rows, NBLK)
    spare = jnp.zeros((BLK, H, HD), jnp.float32)
    key_blocks = jnp.concatenate([key_heads, spare]).reshape(NBLK + 1, BLK, H, HD).transpose(2, 0, 1, 3)
    value_blocks = jnp.concatenate([value_heads, spare]).reshape(NBLK + 1, BLK, H, HD).transpose(2, 0, 1, 3)
    live_blocks = jnp.concatenate([key_live, jnp.zeros((BLK,), jnp.bool_)]).reshape(NBLK + 1, BLK)
    head_index = jnp.arange(H)[None, :, None]
    picked_keys = key_blocks[head_index, chosen].reshape(NBLK - 2, H, 8 * BLK, HD)
    picked_values = value_blocks[head_index, chosen].reshape(NBLK - 2, H, 8 * BLK, HD)
    picked_live = live_blocks[chosen].reshape(NBLK - 2, H, 8 * BLK)
    block_query = query_heads[front:].reshape(NBLK - 2, BLK, H, HD)
    block_scores = low_back(jnp.einsum('bqhd,bhkd->bhqk', block_query, picked_keys, precision=highest))
    block_scores = jnp.where(picked_live[:, :, None, :], block_scores, masked_fill)
    block_probs = low(jax.nn.softmax(block_scores, axis=-1))
    block_out = jnp.einsum('bhqk,bhkd->bqhd', block_probs, picked_values, precision=highest)
    block_out = block_out.reshape(token_count - front, H, HD)
    mixed = low_back(low(jnp.concatenate([global_out, block_out]).reshape(token_count, H * HD)))
    attended = low_back(product(mixed, out_weight) + out_bias)
    residual = window + attended
    normed_two = low(layer_norm(residual, second_gain, second_shift))
    hidden = low_back(product(normed_two, up_weight) + up_bias)
    activated = low(jax.nn.gelu(hidden, approximate=False))
    branch = low_back(product(activated, down_weight) + down_bias)
    return residual + branch

def reference(tokens, lengths, rand_blocks, cotangent, first_gain, first_shift, query_weight, query_bias, key_weight, value_weight, value_bias, out_weight, out_bias, second_gain, second_shift, up_weight, up_bias, down_weight, down_bias):
    params = tuple((item.astype(jnp.float32) for item in (first_gain, first_shift, query_weight, query_bias, key_weight, value_weight, value_bias, out_weight, out_bias, second_gain, second_shift, up_weight, up_bias, down_weight, down_bias)))
    group_size = 4
    token_groups = tokens.astype(jnp.float32).reshape(SEQS // group_size, group_size, LMAX, D)
    cot_groups = cotangent.astype(jnp.float32).reshape(SEQS // group_size, group_size, LMAX, D)
    length_groups = lengths.reshape(SEQS // group_size, group_size)
    rand_groups = rand_blocks.reshape(SEQS // group_size, group_size, NBLK - 2, H, 3)

    def group_pass(totals, items):
        windows, group_lengths, group_rands, group_cots = items

        def forward(window_batch, weights):
            return jax.vmap(window_layer, in_axes=(0, 0, 0, None))(window_batch, group_lengths, group_rands, weights)
        outputs, pullback = jax.vjp(forward, windows, params)
        window_grads, param_grads = pullback(group_cots)
        totals = jax.tree.map(lambda total, piece: total + piece, totals, param_grads)
        return (totals, (outputs.astype(jnp.bfloat16), window_grads))
    start = tuple((jnp.zeros(item.shape, jnp.float32) for item in params))
    totals, (outputs, window_grads) = lax.scan(group_pass, start, (token_groups, length_groups, rand_groups, cot_groups))
    return (outputs.reshape(TOKENS, D), window_grads.reshape(TOKENS, D), totals[0], totals[1], totals[2], totals[3], totals[4], totals[5], totals[6], totals[7], totals[8], totals[9], totals[10], totals[11], totals[12], totals[13], totals[14])
```

```python
import functools

import jax
import jax.numpy as jnp
from jax import lax
from jax.experimental import pallas as pl
from jax.experimental.pallas import tpu as pltpu
from jax.sharding import PartitionSpec as P

H = 12
HD = 64
BLK = 64
NBLK = 16
D = H * HD
QUAD = 4 * HD
NQUAD = H // 4
PICKED = 8 * BLK
FIXED = 5 * BLK

masked_fill = -1e30
bf_type = jnp.bfloat16
f_type = jnp.float32
AXES = ("dp", "fsdp")
VMEM_LIMIT = 63 * 1024 * 1024


def dot_nn(left, right):
    return lax.dot_general(left, right, (((1,), (0,)), ((), ())), preferred_element_type=f_type)


def dot_nt(left, right):
    return lax.dot_general(left, right, (((1,), (1,)), ((), ())), preferred_element_type=f_type)


def dot_tn(left, right):
    return lax.dot_general(left, right, (((0,), (0,)), ((), ())), preferred_element_type=f_type)


def norm_parts(values):
    centre = jnp.mean(values, axis=-1, keepdims=True)
    centred = values - centre
    inverse = lax.rsqrt(jnp.mean(centred * centred, axis=-1, keepdims=True) + 1e-05)
    return centred * inverse, inverse


def norm_back(upstream, gain, unit, inverse):
    scaled = upstream * gain
    first = jnp.mean(scaled, axis=-1, keepdims=True)
    second = jnp.mean(scaled * unit, axis=-1, keepdims=True)
    return inverse * (scaled - first - unit * second)


def lane_heads(width):
    return lax.broadcasted_iota(jnp.int32, (1, width), 1) // HD


def spread_heads(rows):
    heads = lane_heads(QUAD)
    zero = jnp.zeros_like(rows)
    return jnp.concatenate([jnp.where(heads == item, rows, zero) for item in range(4)], axis=0)


def fold_heads(stacked):
    heads = lane_heads(QUAD)
    total = None
    for item in range(4):
        piece = jnp.where(heads == item, stacked[item * BLK : (item + 1) * BLK], 0.0)
        total = piece if total is None else total + piece
    return total


def pick_random(rand_ref, source, target, block, quad):
    upper = lax.broadcasted_iota(jnp.int32, (1, 2 * HD), 1) >= HD
    for slot in range(3):
        for pair in range(2):
            head = quad * 4 + pair * 2
            lanes = pl.ds(quad * QUAD + pair * 2 * HD, 2 * HD)
            first = rand_ref[((block - 2) * H + head) * 3 + slot]
            second = rand_ref[((block - 2) * H + head + 1) * 3 + slot]
            left = source[pl.ds(pl.multiple_of(first * BLK, BLK), BLK), lanes]
            right = source[pl.ds(pl.multiple_of(second * BLK, BLK), BLK), lanes]
            target[FIXED + slot * BLK : FIXED + (slot + 1) * BLK, pair * 2 * HD : (pair + 1) * 2 * HD] = jnp.where(
                upper, right, left
            )


def front_kernel(
    rand_ref,
    x_ref,
    lane_bias_ref,
    global_bias_ref,
    gain_ref,
    shift_ref,
    query_bias_ref,
    value_bias_ref,
    out_bias_ref,
    query_weight_ref,
    key_weight_ref,
    value_weight_ref,
    out_weight_ref,
    normed_ref,
    query_ref,
    key_ref,
    value_ref,
    mixed_ref,
    residual_ref,
    picked_key,
    picked_value,
):
    slots = x_ref.shape[0]
    step = 256

    @pl.loop(0, slots // step)
    def _(turn):
        rows = pl.ds(pl.multiple_of(turn * step, step), step)
        unit, inverse = norm_parts(x_ref[rows, :].astype(f_type))
        normed = (unit * gain_ref[...] + shift_ref[...]).astype(bf_type)
        normed_ref[rows, :] = normed
        query_ref[rows, :] = (
            (dot_nn(normed, query_weight_ref[...]) + query_bias_ref[...]) * 0.125
        ).astype(bf_type)
        key_ref[rows, :] = dot_nn(normed, key_weight_ref[...]).astype(bf_type)
        value_ref[rows, :] = (dot_nn(normed, value_weight_ref[...]) + value_bias_ref[...]).astype(bf_type)

    key_ref[pl.ds(slots, BLK), :] = jnp.zeros((BLK, D), bf_type)
    value_ref[pl.ds(slots, BLK), :] = jnp.zeros((BLK, D), bf_type)

    for quad in range(NQUAD):
        lanes = pl.ds(quad * QUAD, QUAD)

        @pl.loop(0, 2)
        def _(block):
            rows = pl.ds(pl.multiple_of(block * BLK, BLK), BLK)
            query = spread_heads(query_ref[rows, lanes])
            scores = dot_nt(query, key_ref[pl.ds(0, slots), lanes]) + global_bias_ref[...]
            top = jnp.max(scores, axis=-1, keepdims=True)
            powers = jnp.exp(scores - top)
            total = jnp.sum(powers, axis=-1, keepdims=True)
            out = dot_nn(powers.astype(bf_type), value_ref[pl.ds(0, slots), lanes]) / total
            mixed_ref[rows, lanes] = fold_heads(out).astype(bf_type)

        picked_key[0 : 2 * BLK, :] = key_ref[0 : 2 * BLK, lanes]
        picked_value[0 : 2 * BLK, :] = value_ref[0 : 2 * BLK, lanes]

        @pl.loop(2, NBLK)
        def _(block):
            rows = pl.ds(pl.multiple_of(block * BLK, BLK), BLK)
            near = pl.ds(pl.multiple_of((block - 1) * BLK, BLK), 3 * BLK)
            picked_key[2 * BLK : FIXED, :] = key_ref[near, lanes]
            picked_value[2 * BLK : FIXED, :] = value_ref[near, lanes]
            pick_random(rand_ref, key_ref, picked_key, block, quad)
            pick_random(rand_ref, value_ref, picked_value, block, quad)
            query = spread_heads(query_ref[rows, lanes])
            scores = dot_nt(query, picked_key[...])
            bias = lane_bias_ref[(block - 2) * NQUAD + quad]
            scores = jnp.concatenate(
                [scores[item * BLK : (item + 1) * BLK] + bias[item : item + 1] for item in range(4)], axis=0
            )
            top = jnp.max(scores, axis=-1, keepdims=True)
            powers = jnp.exp(scores - top)
            total = jnp.sum(powers, axis=-1, keepdims=True)
            out = dot_nn(powers.astype(bf_type), picked_value[...]) / total
            mixed_ref[rows, lanes] = fold_heads(out).astype(bf_type)

    @pl.loop(0, slots // step)
    def _(turn):
        rows = pl.ds(pl.multiple_of(turn * step, step), step)
        residual_ref[rows, :] = (
            x_ref[rows, :].astype(f_type) + dot_nn(mixed_ref[rows, :], out_weight_ref[...]) + out_bias_ref[...]
        )


ROOT_HALF = 0.7071067811865476
DENSITY = 0.3989422804014327


def feed_kernel(
    residual_ref,
    cot_ref,
    mixed_ref,
    gain_ref,
    shift_ref,
    up_bias_ref,
    down_bias_ref,
    up_weight_ref,
    down_weight_ref,
    out_weight_ref,
    layer_ref,
    up_grad_ref,
    down_grad_ref,
    out_grad_ref,
    grad_resid_ref,
    grad_mixed_ref,
    small_ref,
    up_bias_grad_ref,
    act_ref,
    grad_hidden_ref,
    normed_ref,
    grad_attn_ref,
    branch_acc,
    back_acc,
):
    slots = residual_ref.shape[0]
    hidden_width = up_weight_ref.shape[1]
    step = 256
    part = 512

    small_ref[...] = jnp.zeros(small_ref.shape, f_type)
    up_bias_grad_ref[...] = jnp.zeros(up_bias_grad_ref.shape, f_type)

    @pl.loop(0, slots // step)
    def _(turn):
        rows = pl.ds(pl.multiple_of(turn * step, step), step)
        unit, inverse = norm_parts(residual_ref[rows, :])
        normed = (unit * gain_ref[...] + shift_ref[...]).astype(bf_type)
        normed_ref[rows, :] = normed
        cot = cot_ref[rows, :]
        branch_acc[...] = jnp.zeros(branch_acc.shape, f_type)
        back_acc[...] = jnp.zeros(back_acc.shape, f_type)

        @pl.loop(0, hidden_width // part)
        def _(piece):
            lanes = pl.ds(pl.multiple_of(piece * part, part), part)
            hidden = dot_nn(normed_ref[rows, :], up_weight_ref[:, lanes]) + up_bias_ref[:, lanes]
            cumulative = 0.5 * (1.0 + lax.erf(hidden * ROOT_HALF))
            act = (hidden * cumulative).astype(bf_type)
            act_ref[rows, lanes] = act
            slope = cumulative + hidden * (DENSITY * jnp.exp(-0.5 * hidden * hidden))
            down = down_weight_ref[lanes, :]
            branch_acc[...] += dot_nn(act, down)
            grad_hidden = (dot_nt(cot_ref[rows, :], down) * slope).astype(bf_type)
            grad_hidden_ref[rows, lanes] = grad_hidden
            up_bias_grad_ref[:, lanes] += jnp.sum(grad_hidden.astype(f_type), axis=0, keepdims=True)
            back_acc[...] += dot_nt(grad_hidden, up_weight_ref[:, lanes])

        layer_ref[rows, :] = (residual_ref[rows, :] + branch_acc[...] + down_bias_ref[...]).astype(bf_type)
        unit, inverse = norm_parts(residual_ref[rows, :])
        upstream = back_acc[...]
        wide_cot = cot.astype(f_type)
        grad_resid = wide_cot + norm_back(upstream, gain_ref[...], unit, inverse)
        grad_resid_ref[rows, :] = grad_resid
        grad_attn = grad_resid.astype(bf_type)
        grad_attn_ref[rows, :] = grad_attn
        grad_mixed_ref[rows, :] = dot_nt(grad_attn, out_weight_ref[...]).astype(bf_type)
        small_ref[0:1, :] += jnp.sum(upstream * unit, axis=0, keepdims=True)
        small_ref[1:2, :] += jnp.sum(upstream, axis=0, keepdims=True)
        small_ref[2:3, :] += jnp.sum(wide_cot, axis=0, keepdims=True)
        small_ref[3:4, :] += jnp.sum(grad_attn.astype(f_type), axis=0, keepdims=True)

    tile = 256

    @pl.loop(0, hidden_width // tile)
    def _(piece):
        lanes = pl.ds(pl.multiple_of(piece * tile, tile), tile)
        down_grad_ref[lanes, :] = dot_tn(act_ref[:, lanes], cot_ref[...]).astype(bf_type)

    @pl.loop(0, D // tile)
    def _(piece):
        lanes = pl.ds(pl.multiple_of(piece * tile, tile), tile)
        up_grad_ref[lanes, :] = dot_tn(normed_ref[:, lanes], grad_hidden_ref[...]).astype(bf_type)
        out_grad_ref[lanes, :] = dot_tn(mixed_ref[:, lanes], grad_attn_ref[...]).astype(bf_type)


def soft_back(scores_t, prob_grad_t):
    top = jnp.max(scores_t, axis=0, keepdims=True)
    powers = jnp.exp(scores_t - top)
    inverse = 1.0 / jnp.sum(powers, axis=0, keepdims=True)
    probs = powers * inverse
    delta = jnp.sum(probs * prob_grad_t, axis=0, keepdims=True)
    return probs.astype(bf_type), (probs * (prob_grad_t - delta)).astype(bf_type)


def back_kernel(
    rand_ref,
    length_ref,
    limit_ref,
    query_ref,
    key_ref,
    value_ref,
    grad_mixed_ref,
    normed_ref,
    x_ref,
    grad_resid_ref,
    gain_ref,
    query_weight_ref,
    key_weight_ref,
    value_weight_ref,
    input_grad_ref,
    query_grad_ref,
    key_grad_ref,
    value_grad_ref,
    small_ref,
    picked_key,
    picked_value,
    key_acc,
    value_acc,
    grad_query_ref,
    grad_key_ref,
    grad_value_ref,
):
    slots = x_ref.shape[0]
    key_acc[...] = jnp.zeros(key_acc.shape, f_type)
    value_acc[...] = jnp.zeros(value_acc.shape, f_type)
    small_ref[...] = jnp.zeros(small_ref.shape, f_type)
    length = length_ref[0]
    upper = lax.broadcasted_iota(jnp.int32, (1, 2 * HD), 1) >= HD

    for quad in range(NQUAD):
        lanes = pl.ds(quad * QUAD, QUAD)

        @pl.loop(0, 2)
        def _(block):
            rows = pl.ds(pl.multiple_of(block * BLK, BLK), BLK)
            query = spread_heads(query_ref[rows, lanes])
            grad = spread_heads(grad_mixed_ref[rows, lanes])
            keys = key_ref[pl.ds(0, slots), lanes]
            scores_t = dot_nt(keys, query)
            scores_t = jnp.where(
                lax.broadcasted_iota(jnp.int32, scores_t.shape, 0) < length, scores_t, masked_fill
            )
            prob_grad_t = dot_nt(value_ref[pl.ds(0, slots), lanes], grad)
            probs, dscore = soft_back(scores_t, prob_grad_t)
            key_acc[pl.ds(0, slots), lanes] += dot_nn(dscore, query)
            value_acc[pl.ds(0, slots), lanes] += dot_nn(probs, grad)
            grad_query_ref[rows, lanes] = fold_heads(dot_tn(dscore, keys)).astype(bf_type)

        picked_key[0 : 2 * BLK, :] = key_ref[0 : 2 * BLK, lanes]
        picked_value[0 : 2 * BLK, :] = value_ref[0 : 2 * BLK, lanes]

        @pl.loop(2, NBLK)
        def _(block):
            rows = pl.ds(pl.multiple_of(block * BLK, BLK), BLK)
            near = pl.ds(pl.multiple_of((block - 1) * BLK, BLK), 3 * BLK)
            picked_key[2 * BLK : FIXED, :] = key_ref[near, lanes]
            picked_value[2 * BLK : FIXED, :] = value_ref[near, lanes]
            pick_random(rand_ref, key_ref, picked_key, block, quad)
            pick_random(rand_ref, value_ref, picked_value, block, quad)
            query = spread_heads(query_ref[rows, lanes])
            grad = spread_heads(grad_mixed_ref[rows, lanes])
            scores_t = dot_nt(picked_key[...], query)
            limits = limit_ref[block - 2, :, lanes]
            place = lax.broadcasted_iota(jnp.int32, (BLK, QUAD), 0)
            scores_t = jnp.concatenate(
                [scores_t[0 : 2 * BLK]]
                + [
                    jnp.where(
                        place < limits[item : item + 1], scores_t[item * BLK : (item + 1) * BLK], masked_fill
                    )
                    for item in range(2, 8)
                ],
                axis=0,
            )
            prob_grad_t = dot_nt(picked_value[...], grad)
            probs, dscore = soft_back(scores_t, prob_grad_t)
            grad_query_ref[rows, lanes] = fold_heads(dot_tn(dscore, picked_key[...])).astype(bf_type)
            for acc, piece in ((key_acc, dot_nn(dscore, query)), (value_acc, dot_nn(probs, grad))):
                acc[pl.ds(0, 2 * BLK), lanes] += piece[0 : 2 * BLK]
                acc[near, lanes] += piece[2 * BLK : FIXED]
                for slot in range(3):
                    for pair in range(2):
                        head = quad * 4 + pair * 2
                        pair_lanes = pl.ds(quad * QUAD + pair * 2 * HD, 2 * HD)
                        part = piece[
                            FIXED + slot * BLK : FIXED + (slot + 1) * BLK, pair * 2 * HD : (pair + 1) * 2 * HD
                        ]
                        first = rand_ref[((block - 2) * H + head) * 3 + slot]
                        second = rand_ref[((block - 2) * H + head + 1) * 3 + slot]
                        acc[pl.ds(pl.multiple_of(first * BLK, BLK), BLK), pair_lanes] += jnp.where(
                            upper, 0.0, part
                        )
                        acc[pl.ds(pl.multiple_of(second * BLK, BLK), BLK), pair_lanes] += jnp.where(
                            upper, part, 0.0
                        )

    step = 256

    @pl.loop(0, slots // step)
    def _(turn):
        rows = pl.ds(pl.multiple_of(turn * step, step), step)
        grad_query = grad_query_ref[rows, :]
        grad_key = key_acc[rows, :].astype(bf_type)
        grad_value = value_acc[rows, :].astype(bf_type)
        grad_key_ref[rows, :] = grad_key
        grad_value_ref[rows, :] = grad_value
        upstream = (
            dot_nt(grad_query, query_weight_ref[...]) * 0.125
            + dot_nt(grad_key, key_weight_ref[...])
            + dot_nt(grad_value, value_weight_ref[...])
        )
        unit, inverse = norm_parts(x_ref[rows, :].astype(f_type))
        input_grad_ref[rows, :] = grad_resid_ref[rows, :] + norm_back(upstream, gain_ref[...], unit, inverse)
        small_ref[0:1, :] += jnp.sum(upstream * unit, axis=0, keepdims=True)
        small_ref[1:2, :] += jnp.sum(upstream, axis=0, keepdims=True)
        small_ref[2:3, :] += jnp.sum(grad_query.astype(f_type), axis=0, keepdims=True) * 0.125
        small_ref[3:4, :] += jnp.sum(grad_value.astype(f_type), axis=0, keepdims=True)

    tile = 256

    @pl.loop(0, D // tile)
    def _(piece):
        lanes = pl.ds(pl.multiple_of(piece * tile, tile), tile)
        normed = normed_ref[:, lanes]
        query_grad_ref[lanes, :] = (dot_tn(normed, grad_query_ref[...]) * 0.125).astype(bf_type)
        key_grad_ref[lanes, :] = dot_tn(normed, grad_key_ref[...]).astype(bf_type)
        value_grad_ref[lanes, :] = dot_tn(normed, grad_value_ref[...]).astype(bf_type)


def shape(dims, kind):
    return jax.ShapeDtypeStruct(dims, kind)


def in_vmem(count):
    return [pl.BlockSpec(memory_space=pltpu.VMEM)] * count


def in_smem(count):
    return [pl.BlockSpec(memory_space=pltpu.SMEM)] * count


def masks(length, rand_rows):
    later = jnp.arange(2, NBLK, dtype=jnp.int32)
    fixed = jnp.stack([jnp.zeros_like(later), jnp.ones_like(later), later - 1, later, later + 1], axis=-1)
    fixed = jnp.broadcast_to(fixed[:, None, :], (NBLK - 2, H, 5))
    chosen = jnp.concatenate([fixed, rand_rows], axis=-1)
    limits = length - chosen * BLK
    limits = jnp.where(chosen >= NBLK, 0, limits)
    live = jnp.arange(BLK, dtype=jnp.int32) < limits[..., None]
    lane_bias = jnp.where(live, 0.0, masked_fill).astype(f_type).reshape((NBLK - 2) * NQUAD, 4, PICKED)
    limit_rows = jnp.repeat(limits.transpose(0, 2, 1), HD, axis=2)
    global_bias = jnp.where(jnp.arange(NBLK * BLK) < length, 0.0, masked_fill).astype(f_type)[None]
    return lane_bias, global_bias, limit_rows


def front_call(rand_flat, window, lane_bias, global_bias, vectors, weights):
    slots = window.shape[0]
    return pl.pallas_call(
        front_kernel,
        out_shape=(
            shape((slots, D), bf_type),
            shape((slots, D), bf_type),
            shape((slots + BLK, D), bf_type),
            shape((slots + BLK, D), bf_type),
            shape((slots, D), bf_type),
            shape((slots, D), f_type),
        ),
        in_specs=in_smem(1) + in_vmem(12),
        out_specs=tuple(in_vmem(6)),
        scratch_shapes=[pltpu.VMEM((PICKED, QUAD), bf_type)] * 2,
        compiler_params=pltpu.CompilerParams(vmem_limit_bytes=VMEM_LIMIT),
        name="front",
    )(rand_flat, window, lane_bias, global_bias, *vectors, *weights)


def feed_call(residual, cotangent, mixed, vectors, weights):
    slots = residual.shape[0]
    width = weights[0].shape[1]
    return pl.pallas_call(
        feed_kernel,
        out_shape=(
            shape((slots, D), bf_type),
            shape((D, width), bf_type),
            shape((width, D), bf_type),
            shape((D, D), bf_type),
            shape((slots, D), f_type),
            shape((slots, D), bf_type),
            shape((8, D), f_type),
            shape((1, width), f_type),
        ),
        in_specs=in_vmem(10),
        out_specs=tuple(in_vmem(8)),
        scratch_shapes=[
            pltpu.VMEM((slots, width), bf_type),
            pltpu.VMEM((slots, width), bf_type),
            pltpu.VMEM((slots, D), bf_type),
            pltpu.VMEM((slots, D), bf_type),
            pltpu.VMEM((256, D), f_type),
            pltpu.VMEM((256, D), f_type),
        ],
        compiler_params=pltpu.CompilerParams(vmem_limit_bytes=VMEM_LIMIT),
        name="feed",
    )(residual, cotangent, mixed, *vectors, *weights)


def back_call(rand_flat, length, limits, query, key, value, grad_mixed, normed, window, grad_resid, gain, weights):
    slots = window.shape[0]
    return pl.pallas_call(
        back_kernel,
        out_shape=(
            shape((slots, D), f_type),
            shape((D, D), bf_type),
            shape((D, D), bf_type),
            shape((D, D), bf_type),
            shape((8, D), f_type),
        ),
        in_specs=in_smem(2) + in_vmem(12),
        out_specs=tuple(in_vmem(5)),
        scratch_shapes=[
            pltpu.VMEM((PICKED, QUAD), bf_type),
            pltpu.VMEM((PICKED, QUAD), bf_type),
            pltpu.VMEM((slots + BLK, D), f_type),
            pltpu.VMEM((slots + BLK, D), f_type),
            pltpu.VMEM((slots, D), bf_type),
            pltpu.VMEM((slots, D), bf_type),
            pltpu.VMEM((slots, D), bf_type),
        ],
        compiler_params=pltpu.CompilerParams(vmem_limit_bytes=VMEM_LIMIT),
        name="back",
    )(rand_flat, length, limits, query, key, value, grad_mixed, normed, window, grad_resid, gain, *weights)


def window_pass(window, length, rand_rows, cotangent, params):
    (
        first_gain,
        first_shift,
        query_weight,
        query_bias,
        key_weight,
        value_weight,
        value_bias,
        out_weight,
        out_bias,
        second_gain,
        second_shift,
        up_weight,
        up_bias,
        down_weight,
        down_bias,
    ) = params
    lane_bias, global_bias, limits = masks(length[0], rand_rows)
    rand_flat = rand_rows.reshape(-1)
    normed, query, key, value, mixed, residual = front_call(
        rand_flat,
        window,
        lane_bias,
        global_bias,
        (first_gain, first_shift, query_bias, value_bias, out_bias),
        (query_weight, key_weight, value_weight, out_weight),
    )
    layer_out, up_grad, down_grad, out_grad, grad_resid, grad_mixed, feed_small, up_bias_grad = feed_call(
        residual,
        cotangent,
        mixed,
        (second_gain, second_shift, up_bias, down_bias),
        (up_weight, down_weight, out_weight),
    )
    input_grad, query_grad, key_grad, value_grad, back_small = back_call(
        rand_flat,
        length,
        limits,
        query,
        key,
        value,
        grad_mixed,
        normed,
        window,
        grad_resid,
        first_gain,
        (query_weight, key_weight, value_weight),
    )
    grads = (
        back_small[0],
        back_small[1],
        query_grad,
        back_small[2],
        key_grad,
        value_grad,
        back_small[3],
        out_grad,
        feed_small[3],
        feed_small[0],
        feed_small[1],
        up_grad,
        up_bias_grad[0],
        down_grad,
        feed_small[2],
    )
    return layer_out, input_grad, grads


NARROW = (0, 1, 3, 6, 8, 9, 10, 14)


def body(tokens, lengths, rand_blocks, cotangent, *shards):
    rows = shards[0].shape[0]
    narrow = jnp.stack([shards[item] for item in NARROW], axis=1)
    wide_bias = shards[12].reshape(rows, -1)
    spare = jnp.zeros((rows, 128 - len(NARROW) - wide_bias.shape[1]), bf_type)
    first = jnp.concatenate([shards[2], shards[4], shards[5], shards[7], narrow, wide_bias, spare], axis=1)
    gathered = lax.all_gather(first, AXES, axis=0, tiled=True)
    up_weight = lax.all_gather(shards[11], AXES, axis=0, tiled=True)
    down_weight = lax.all_gather(shards[13], AXES, axis=0, tiled=True)
    query_weight, key_weight, value_weight, out_weight = (gathered[:, D * item : D * (item + 1)] for item in range(4))
    tail = gathered[:, 4 * D :].astype(f_type)
    whole = [None] * 15
    for place, item in enumerate(NARROW):
        whole[item] = tail[:, place][None]
    whole[12] = tail[:, len(NARROW) : len(NARROW) + wide_bias.shape[1]].reshape(1, -1)
    whole[2], whole[4], whole[5], whole[7] = query_weight, key_weight, value_weight, out_weight
    whole[11], whole[13] = up_weight, down_weight

    windows = lengths.shape[0]
    slots = tokens.shape[0] // windows
    layers, inputs, totals = [], [], None
    for item in range(windows):
        part = slice(item * slots, (item + 1) * slots)
        layer_out, input_grad, grads = window_pass(
            tokens[part], lengths[item : item + 1], rand_blocks[item], cotangent[part], whole
        )
        layers.append(layer_out)
        inputs.append(input_grad)
        totals = grads if totals is None else tuple(a + b for a, b in zip(totals, grads))
    layer_out = layers[0] if windows == 1 else jnp.concatenate(layers)
    input_grad = inputs[0] if windows == 1 else jnp.concatenate(inputs)

    def scatter(values):
        return lax.psum_scatter(values.astype(bf_type), AXES, scatter_dimension=0, tiled=True).astype(f_type)

    owned_down = scatter(totals[13])
    owned_up = scatter(totals[11])
    narrow_grads = jnp.stack([totals[item] for item in NARROW], axis=1)
    wide_grads = totals[12].reshape(D, -1)
    spare = jnp.zeros((D, 128 - len(NARROW) - wide_grads.shape[1]), f_type)
    small = jnp.concatenate([narrow_grads, wide_grads, spare], axis=1).astype(bf_type)
    owned = scatter(jnp.concatenate([totals[2], totals[4], totals[5], totals[7], small], axis=1))
    result = [None] * 15
    for place, item in enumerate((2, 4, 5, 7)):
        result[item] = owned[:, D * place : D * (place + 1)]
    for place, item in enumerate(NARROW):
        result[item] = owned[:, 4 * D + place]
    start = 4 * D + len(NARROW)
    result[12] = owned[:, start : start + wide_bias.shape[1]].reshape(-1)
    result[11], result[13] = owned_up, owned_down
    return (layer_out, input_grad, *result)


def solution(mesh):
    row = P(AXES, None)
    flat = P(AXES)
    params = (flat, flat, row, flat, row, row, flat, row, flat, flat, flat, row, flat, row, flat)
    in_specs = (row, flat, P(AXES, None, None, None), row) + params
    out_specs = (row, row) + params
    return jax.shard_map(body, mesh=mesh, in_specs=in_specs, out_specs=out_specs, check_vma=False)
```
